32 devices in a mesh: row: 8 (over y, x, core), col: 4 (over z).
Axes of the slice: x: 2, y: 2, z: 4, core: 2. Of those that a mesh axis runs over, the one named last changes fastest.
Arguments:
- iterate_t: bfloat16 [8, 4, 1024, 32768], P(None, 'col', None, 'row'), may hold values from -0.03125 to 0.03125
- vectors: bfloat16 [32768, 256], P(('row', 'col')), may hold values from -6 to 6
- old_factor_t: bfloat16 [512, 32768], P('col', 'row'), may hold values from -5 to 5
Outputs:
- panel: float32 [32768, 256], P(('row', 'col'))
- basis: float32 [768, 32768], P('col', 'row')
The draws below stay inside these ranges and needn't reach their ends.
All inputs are finite; a program needn't handle non-finite values.
Results may differ from the reference program's by a relative error of at most 0.0013.
Values may be sent and summed in bfloat16 or wider, within the bound.
No kernel may reach another device: no remote copies, remote signals or barrier semaphores. Data moves between devices by JAX's collectives and lax.ppermute only.
A program may use at most 192 MiB of HBM per device.

```python
import jax
import jax.numpy as jnp
from jax import lax

NSTATE = 32768
PANEL = 256
OLD = 512
FACTOR = 768
STRIPS = 8
GROUPS = 4
CB = 1024


def draw_old_factor_t(key, part):
    noise_key, shared_key = jax.random.split(jax.random.fold_in(key, 7))
    noise = jax.random.truncated_normal(noise_key, -4.0, 4.0, (OLD, NSTATE), jnp.float32)
    shared = jax.random.normal(shared_key, (1, NSTATE), jnp.float32)
    values = jnp.clip(noise + 0.6 * shared, -5.0, 5.0)
    return values.astype(jnp.bfloat16)


def steps_of(own_key, dims, cuts, smallest, high):
    level, own = 1.0, jax.random.fold_in(own_key, 6)
    for axis_at, blocks in cuts:
        draws = jnp.exp(jax.random.uniform(jax.random.fold_in(own, axis_at), (blocks,), jnp.float32, smallest / len(cuts), high / len(cuts)))
        level = level * jnp.repeat(draws, dims[axis_at] // blocks).reshape([-1 if axis == axis_at else 1 for axis in range(len(dims))])
    return level


def gaussian(stream_key, extent, spread, bound, cuts=(), kind=jnp.bfloat16):
    loudness = steps_of(stream_key, extent, cuts, -0.22, 0.18) if cuts else 1.0
    entries = jax.random.normal(stream_key, extent, jnp.float32) * spread * loudness
    return jnp.minimum(jnp.maximum(entries, -bound), bound).astype(kind)


def setup_inputs(seed: int = 0) -> dict:
    streams_of = jax.random.split(jax.random.key(seed), 4)
    return {
        "iterate_t": gaussian(streams_of[0], (STRIPS, GROUPS, CB, NSTATE), NSTATE ** -0.5, 0.03125, ((1, 4), (3, 8))),
        "vectors": gaussian(streams_of[1], (NSTATE, PANEL), 1.0, 6.0, ((0, 32),)),
        "old_factor_t": draw_old_factor_t(jax.random.fold_in(streams_of[3], 71), 0),
    }


def reference(iterate_t, vectors, old_factor_t):
    flat_iterate = iterate_t.reshape(NSTATE, NSTATE)
    slab_width = min(1024, NSTATE)

    def apply_iterate(vector):
        vector_full = vector.astype(jnp.float32)

        def one_slab(first_row):
            column_slab = lax.dynamic_slice_in_dim(flat_iterate, first_row, slab_width, 1).astype(jnp.float32)
            return lax.dot_general(column_slab, vector_full, (((0,), (0,)), ((), ())), precision=lax.Precision.HIGHEST)
        slab_starts = (jnp.arange(NSTATE // slab_width) * slab_width).astype(jnp.int32)
        return lax.map(one_slab, slab_starts).reshape(NSTATE, PANEL)
    first_full = apply_iterate(vectors)
    second = apply_iterate(first_full.astype(jnp.bfloat16)).astype(jnp.bfloat16)
    panel = 1.5 * first_full - 0.5 * apply_iterate(second)
    old_full = old_factor_t.astype(jnp.float32)
    old_old = jnp.dot(old_full, old_full.T, precision=lax.Precision.HIGHEST)
    old_panel = jnp.dot(old_full, panel, precision=lax.Precision.HIGHEST)
    panel_panel = jnp.dot(panel.T, panel, precision=lax.Precision.HIGHEST)
    gram = jnp.concatenate([jnp.concatenate([old_old, old_panel], 1), jnp.concatenate([old_panel.T, panel_panel], 1)], 0) * (1.0 / NSTATE)
    lower_factor = jnp.linalg.cholesky(gram)
    identity = jnp.eye(FACTOR, dtype=jnp.float32)
    inverse = jax.scipy.linalg.solve_triangular(lower_factor, identity, lower=True)
    basis = jnp.dot(inverse[:, :OLD], old_full, precision=lax.Precision.HIGHEST)
    basis = basis + jnp.dot(inverse[:, OLD:], panel.T, precision=lax.Precision.HIGHEST)
    return (panel, basis)
```

```python
import functools

import jax
import jax.numpy as jnp
from jax import lax
from jax.experimental import pallas as pl
from jax.experimental.pallas import tpu as pltpu
from jax.sharding import PartitionSpec as P


HIGHEST = lax.Precision.HIGHEST
TILE = 8
LANES = 128


def swap(value, axis, bit):
    size = lax.axis_size(axis)
    return lax.ppermute(value, axis, [(i, i ^ bit) for i in range(size)])


def bits_of(size, first=1):
    bits, bit = [], first
    while bit < size:
        bits.append(bit)
        bit *= 2
    return bits


def has_bit(axis, bit):
    return (lax.axis_index(axis) // bit) % 2


def join(own, other, axis, bit, dim):
    low = jnp.concatenate([own, other], dim)
    high = jnp.concatenate([other, own], dim)
    return jnp.where(has_bit(axis, bit) == 0, low, high)


def gather_rows(value):
    size = lax.axis_size("row")
    chip_bits = bits_of(size, 2)
    half = value.shape[0] // 2
    turn = len(chip_bits) // 2
    parts = []
    for which in range(2):
        piece = value[which * half : (which + 1) * half]
        piece = piece.reshape((1,) * len(chip_bits) + piece.shape)
        order = chip_bits[turn:] + chip_bits[:turn] if which else chip_bits
        for bit in order:
            dim = len(chip_bits) - 1 - chip_bits.index(bit)
            piece = join(piece, swap(piece, "row", bit), "row", bit, dim)
        parts.append(piece.reshape(size // 2, 1, 1, half, value.shape[1]))
    own = jnp.concatenate(parts, 2)
    return join(own, swap(own, "row", 1), "row", 1, 1).reshape(-1, value.shape[1])


def scatter_cols(block_of, wire):
    size = lax.axis_size("col")
    here = lax.axis_index("col")
    sums = {}

    def take(mask):
        if mask not in sums:
            sums[mask] = block_of(here ^ mask)
        return sums[mask]

    bits = bits_of(size)
    for bit in bits:
        masks = [m for m in range(size) if m % bit == 0 and m & bit]
        for mask in sorted(masks, reverse=True):
            arrived = swap(take(mask).astype(wire), "col", bit)
            kept = take(mask ^ bit)
            sums[mask ^ bit] = kept + arrived.astype(jnp.float32)
    return take(0)


def keep_half(value, axis, bit):
    half = value.shape[0] // 2
    mine = has_bit(axis, bit)
    keep = lax.dynamic_slice_in_dim(value, mine * half, half, 0)
    send = lax.dynamic_slice_in_dim(value, (1 - mine) * half, half, 0)
    return keep + swap(send, axis, bit)


def sum_over(value, over_cols):
    size = lax.axis_size("row")
    chip_bits = bits_of(size, 2)
    turn = len(chip_bits) // 2
    mine = keep_half(value, "row", 1)
    half = mine.shape[0] // 2
    orders = [chip_bits, chip_bits[turn:] + chip_bits[:turn]]
    parts = [mine[:half], mine[half:]]
    for step in range(len(chip_bits)):
        parts = [keep_half(part, "row", order[step]) for part, order in zip(parts, orders)]
    if over_cols:
        both = jnp.concatenate(parts, 0)
        for bit in bits_of(lax.axis_size("col")):
            both = both + swap(both, "col", bit)
        parts = [both[: both.shape[0] // 2], both[both.shape[0] // 2 :]]
    for step in reversed(range(len(chip_bits))):
        parts = [
            join(part, swap(part, "row", order[step]), "row", order[step], 0)
            for part, order in zip(parts, orders)
        ]
    mine = jnp.concatenate(parts, 0)
    return join(mine, swap(mine, "row", 1), "row", 1, 0)


def eliminate(block):
    groups = LANES // TILE
    left = [block[g * TILE : (g + 1) * TILE] for g in range(groups)]
    lane = lax.broadcasted_iota(jnp.int32, (TILE, LANES), 1)
    sub = lax.broadcasted_iota(jnp.int32, (TILE, LANES), 0)
    right = [jnp.where(lane == sub + g * TILE, 1.0, 0.0) for g in range(groups)]
    pivots = [jnp.zeros((TILE, LANES), jnp.float32) for _ in range(groups)]
    for j in range(LANES):
        top, s = j // TILE, j % TILE
        row_left = jnp.broadcast_to(left[top][s : s + 1], (TILE, LANES))
        row_right = jnp.broadcast_to(right[top][s : s + 1], (TILE, LANES))
        pivot = jnp.broadcast_to(row_left[:, j : j + 1], (TILE, LANES))
        inverse = 1.0 / pivot
        row_left = row_left * inverse
        row_right = row_right * inverse
        pivots[top] = jnp.where(sub == s, pivot, pivots[top])
        for g in range(top, groups):
            column = jnp.broadcast_to(left[g][:, j : j + 1], (TILE, LANES))
            if g == top:
                column = jnp.where(sub > s, column, 0.0)
            left[g] = left[g] - column * row_left
            right[g] = right[g] - column * row_right
    return jnp.concatenate([right[g] / jnp.sqrt(pivots[g]) for g in range(groups)], 0)


def dot32(a, b, dims):
    return lax.dot_general(a, b, (dims, ((), ())), precision=HIGHEST, preferred_element_type=jnp.float32)


def invert_factor(left, right):
    size = left.shape[0]
    for start in range(0, size, LANES):
        stop = start + LANES
        diagonal = eliminate(left[start:stop, start:stop])
        right_rows = dot32(diagonal, right[start:stop, :stop], ((1,), (0,)))
        right[start:stop, :stop] = right_rows
        if stop < size:
            left_rows = dot32(diagonal, left[start:stop, stop:], ((1,), (0,)))
            left[stop:, stop:] = left[stop:, stop:] - dot32(left_rows, left_rows, ((0,), (0,)))
            right[stop:, :stop] = right[stop:, :stop] - dot32(left_rows, right_rows, ((0,), (0,)))


def identity_into(ref):
    shape = ref.shape
    ref[...] = jnp.where(
        lax.broadcasted_iota(jnp.int32, shape, 0) == lax.broadcasted_iota(jnp.int32, shape, 1), 1.0, 0.0
    )


def first_factor_kernel(gram_ref, out_ref, left):
    left[...] = gram_ref[...]
    identity_into(out_ref)
    invert_factor(left, out_ref)


def first_factor(gram):
    return pl.pallas_call(
        first_factor_kernel,
        out_shape=jax.ShapeDtypeStruct(gram.shape, jnp.float32),
        scratch_shapes=[pltpu.VMEM(gram.shape, jnp.float32)],
        cost_estimate=pl.CostEstimate(flops=2 * gram.shape[0] ** 3, bytes_accessed=1 << 27, transcendentals=0),
    )(gram)


def last_factor_kernel(inverse_ref, gram_ref, out_ref, left, right):
    old = inverse_ref.shape[0]
    upper = dot32(inverse_ref[...], gram_ref[:old], ((1,), (0,)))
    left[...] = gram_ref[old:] - dot32(upper, upper, ((0,), (0,)))
    below = dot32(upper, inverse_ref[...], ((0,), (0,)))
    identity_into(right)
    invert_factor(left, right)
    out_ref[:old, :old] = inverse_ref[...]
    out_ref[:old, old:] = jnp.zeros((old, left.shape[0]), jnp.float32)
    out_ref[old:, :old] = -dot32(right[...], below, ((1,), (0,)))
    out_ref[old:, old:] = right[...]


def last_factor(inverse, gram_columns):
    total, new = gram_columns.shape
    return pl.pallas_call(
        last_factor_kernel,
        out_shape=jax.ShapeDtypeStruct((total, total), jnp.float32),
        scratch_shapes=[pltpu.VMEM((new, new), jnp.float32)] * 2,
        cost_estimate=pl.CostEstimate(flops=2 * total**3, bytes_accessed=1 << 26, transcendentals=0),
    )(inverse, gram_columns)


def body(iterate_t, vectors, old_factor_t):
    flat_iterate = iterate_t.reshape(-1, iterate_t.shape[-1])
    rows, groups = lax.axis_size("row"), lax.axis_size("col")
    column = lax.axis_index("col")
    share = vectors.shape[0]
    scale_gram = 1.0 / (rows * groups * share)

    def apply_iterate(vector, wire):
        gathered = gather_rows(vector)

        def block_of(target):
            part = lax.dynamic_slice_in_dim(flat_iterate, target * share, share, 1)
            return lax.optimization_barrier(
                lax.dot_general(
                    part, gathered, (((0,), (0,)), ((), ())), preferred_element_type=jnp.float32
                )
            )

        return scatter_cols(block_of, wire)

    old_gathered = lax.all_gather(old_factor_t, "col", axis=0, tiled=True)
    old_old = lax.dot_general(
        old_gathered, old_gathered, (((1,), (1,)), ((), ())), preferred_element_type=jnp.float32
    )
    old_inverse = first_factor(sum_over(old_old * scale_gram, False))
    old_full = old_gathered.astype(jnp.float32)
    old_here = lax.dynamic_slice_in_dim(old_gathered, column * share, share, 1).astype(jnp.float32)

    first_full = apply_iterate(vectors, jnp.float32)
    second = apply_iterate(first_full.astype(jnp.bfloat16), jnp.bfloat16).astype(jnp.bfloat16)
    panel = 1.5 * first_full - 0.5 * apply_iterate(second, jnp.bfloat16)

    old_panel = jnp.dot(old_here, panel, precision=HIGHEST)
    panel_panel = lax.dot_general(panel, panel, (((0,), (0,)), ((), ())), precision=HIGHEST)
    gram_columns = sum_over(jnp.concatenate([old_panel, panel_panel], 0) * scale_gram, True)
    panel_gathered = lax.all_gather(panel, "col", axis=0, tiled=True)
    inverse = last_factor(old_inverse, gram_columns)
    basis_share = inverse.shape[0] // groups
    inverse_rows = lax.dynamic_slice_in_dim(inverse, column * basis_share, basis_share, 0)
    old_count = old_gathered.shape[0]
    basis = jnp.dot(inverse_rows[:, :old_count], old_full, precision=HIGHEST)
    basis = basis + lax.dot_general(
        inverse_rows[:, old_count:], panel_gathered, (((1,), (1,)), ((), ())), precision=HIGHEST
    )
    return (panel, basis)


def solution(mesh):
    return jax.shard_map(
        body,
        mesh=mesh,
        in_specs=(P(None, "col", None, "row"), P(("row", "col"), None), P("col", "row")),
        out_specs=(P(("row", "col"), None), P("col", "row")),
        check_vma=False,
    )
```

```python
import jax
import jax.numpy as jnp
from jax import lax
from jax.experimental import pallas as pl
from jax.experimental.pallas import tpu as pltpu
from jax.sharding import PartitionSpec as P


HIGHEST = lax.Precision.HIGHEST
HIGH = lax.Precision.HIGH
TILE = 8
LANES = 128


def swap(value, axis, bit):
    size = lax.axis_size(axis)
    return lax.ppermute(value, axis, [(i, i ^ bit) for i in range(size)])


def bits_of(size, first=1):
    bits, bit = [], first
    while bit < size:
        bits.append(bit)
        bit *= 2
    return bits


def has_bit(axis, bit):
    return (lax.axis_index(axis) // bit) % 2


def join(own, other, axis, bit, dim):
    low = jnp.concatenate([own, other], dim)
    high = jnp.concatenate([other, own], dim)
    return jnp.where(has_bit(axis, bit) == 0, low, high)


def gather_rows(value):
    size = lax.axis_size("row")
    chip_bits = bits_of(size, 2)
    half = value.shape[0] // 2
    turn = len(chip_bits) // 2
    parts = []
    for which in range(2):
        piece = value[which * half : (which + 1) * half]
        piece = piece.reshape((1,) * len(chip_bits) + piece.shape)
        order = chip_bits[turn:] + chip_bits[:turn] if which else chip_bits
        for bit in order:
            dim = len(chip_bits) - 1 - chip_bits.index(bit)
            piece = join(piece, swap(piece, "row", bit), "row", bit, dim)
        parts.append(piece.reshape(size // 2, 1, 1, half, value.shape[1]))
    own = jnp.concatenate(parts, 2)
    return join(own, swap(own, "row", 1), "row", 1, 1).reshape(-1, value.shape[1])


def scatter_cols(block_of, here, wire):
    size = lax.axis_size("col")
    sums = {}

    def take(mask):
        if mask not in sums:
            sums[mask] = block_of(here ^ mask if mask else here)
        return sums[mask]

    bits = bits_of(size)
    for bit in bits:
        masks = [m for m in range(size) if m % bit == 0 and m & bit]
        for mask in sorted(masks, reverse=True):
            arrived = swap(take(mask).astype(wire), "col", bit)
            kept = take(mask ^ bit)
            sums[mask ^ bit] = kept + arrived.astype(jnp.float32)
    return take(0)


def keep_half(value, axis, bit):
    half = value.shape[0] // 2
    mine = has_bit(axis, bit)
    keep = lax.dynamic_slice_in_dim(value, mine * half, half, 0)
    send = lax.dynamic_slice_in_dim(value, (1 - mine) * half, half, 0)
    return keep + swap(send, axis, bit)


def sum_all(value):
    size = lax.axis_size("row")
    chip_bits = bits_of(size, 2)
    turn = len(chip_bits) // 2
    mine = keep_half(value, "row", 1)
    half = mine.shape[0] // 2
    orders = [chip_bits, chip_bits[turn:] + chip_bits[:turn]]
    parts = [mine[:half], mine[half:]]
    for step in range(len(chip_bits)):
        parts = [keep_half(part, "row", order[step]) for part, order in zip(parts, orders)]
    both = jnp.concatenate(parts, 0)
    for bit in bits_of(lax.axis_size("col")):
        both = both + swap(both, "col", bit)
    parts = [both[: both.shape[0] // 2], both[both.shape[0] // 2 :]]
    for step in reversed(range(len(chip_bits))):
        parts = [
            join(part, swap(part, "row", order[step]), "row", order[step], 0)
            for part, order in zip(parts, orders)
        ]
    mine = jnp.concatenate(parts, 0)
    return join(mine, swap(mine, "row", 1), "row", 1, 0)


def eliminate(block):
    groups = LANES // TILE
    wide = (LANES, LANES)
    diagonal = lax.broadcasted_iota(jnp.int32, wide, 0) == lax.broadcasted_iota(jnp.int32, wide, 1)
    only = jnp.where(diagonal, block, 0.0)
    scale_row = 1.0 / jnp.sqrt(jnp.sum(only, axis=0, keepdims=True))
    scale_column = 1.0 / jnp.sqrt(jnp.sum(only, axis=1, keepdims=True))
    block = block * scale_row * scale_column
    start = jnp.where(diagonal, jnp.broadcast_to(scale_row, wide), 0.0)
    left = [block[g * TILE : (g + 1) * TILE] for g in range(groups)]
    right = [start[g * TILE : (g + 1) * TILE] for g in range(groups)]
    full = (TILE, LANES)
    sub = lax.broadcasted_iota(jnp.int32, full, 0)
    done = []
    for top in range(groups):
        rows = jnp.zeros(full, jnp.float32)
        for s in range(0, TILE, 2):
            j = top * TILE + s
            zero = jnp.broadcast_to(left[top][:, j : j + 1], full)
            one = jnp.broadcast_to(left[top][:, j + 1 : j + 2], full)
            p00 = jnp.broadcast_to(zero[s : s + 1], full)
            p10 = jnp.broadcast_to(zero[s + 1 : s + 2], full)
            p11 = jnp.broadcast_to(one[s + 1 : s + 2], full)
            det = p00 * p11 - p10 * p10
            inverse = 1.0 / det
            m00, m10, m11 = p11 * inverse, p10 * inverse, p00 * inverse
            l0 = jnp.broadcast_to(left[top][s : s + 1], full)
            l1 = jnp.broadcast_to(left[top][s + 1 : s + 2], full)
            r0 = jnp.broadcast_to(right[top][s : s + 1], full)
            r1 = jnp.broadcast_to(right[top][s + 1 : s + 2], full)
            lu0, lu1 = m00 * l0 - m10 * l1, m11 * l1 - m10 * l0
            ru0, ru1 = m00 * r0 - m10 * r1, m11 * r1 - m10 * r0
            for g in range(top, groups):
                if g == top:
                    c0 = jnp.where(sub > s + 1, zero, 0.0)
                    c1 = jnp.where(sub > s + 1, one, 0.0)
                else:
                    c0 = jnp.broadcast_to(left[g][:, j : j + 1], full)
                    c1 = jnp.broadcast_to(left[g][:, j + 1 : j + 2], full)
                left[g] = left[g] - (c0 * lu0 + c1 * lu1)
                right[g] = right[g] - (c0 * ru0 + c1 * ru1)
            rows = jnp.where(sub == s, r0 / jnp.sqrt(p00), rows)
            rows = jnp.where(sub == s + 1, (p00 * r1 - p10 * r0) / jnp.sqrt(p00 * det), rows)
        done.append(rows)
    return jnp.concatenate(done, 0)


def dot32(a, b, dims):
    return lax.dot_general(a, b, (dims, ((), ())), precision=HIGHEST, preferred_element_type=jnp.float32)


def invert_factor(left, right, first, last):
    size = left.shape[0]
    for start in range(first, last, LANES):
        stop = start + LANES
        diagonal = eliminate(left[start:stop, start:stop])
        right_rows = dot32(diagonal, right[start:stop, :stop], ((1,), (0,)))
        right[start:stop, :stop] = right_rows
        if stop < size:
            left_rows = dot32(diagonal, left[start:stop, stop:], ((1,), (0,)))
            left[stop:, stop:] = left[stop:, stop:] - dot32(left_rows, left_rows, ((0,), (0,)))
            right[stop:, :stop] = right[stop:, :stop] - dot32(left_rows, right_rows, ((0,), (0,)))


def identity_into(ref):
    shape = ref.shape
    ref[...] = jnp.where(
        lax.broadcasted_iota(jnp.int32, shape, 0) == lax.broadcasted_iota(jnp.int32, shape, 1), 1.0, 0.0
    )


def begin_factor_kernel(gram_ref, left, right):
    left[...] = gram_ref[...]
    identity_into(right)
    invert_factor(left, right, 0, left.shape[0] // 2)


def begin_factor(gram):
    size = gram.shape[0]
    return pl.pallas_call(
        begin_factor_kernel,
        out_shape=[jax.ShapeDtypeStruct(gram.shape, jnp.float32)] * 2,
        cost_estimate=pl.CostEstimate(flops=2 * size**3, bytes_accessed=1 << 26, transcendentals=0),
    )(gram)


def end_factor_kernel(left_ref, right_ref, out_ref, left):
    left[...] = left_ref[...]
    out_ref[...] = right_ref[...]
    invert_factor(left, out_ref, left.shape[0] // 2, left.shape[0])


def end_factor(left, right):
    size = left.shape[0]
    return pl.pallas_call(
        end_factor_kernel,
        out_shape=jax.ShapeDtypeStruct(left.shape, jnp.float32),
        scratch_shapes=[pltpu.VMEM(left.shape, jnp.float32)],
        cost_estimate=pl.CostEstimate(flops=2 * size**3, bytes_accessed=1 << 26, transcendentals=0),
    )(left, right)


def last_factor_kernel(inverse_ref, gram_ref, out_ref, left, right):
    old = inverse_ref.shape[0]
    upper = dot32(inverse_ref[...], gram_ref[:old], ((1,), (0,)))
    left[...] = gram_ref[old:] - dot32(upper, upper, ((0,), (0,)))
    identity_into(right)
    invert_factor(left, right, 0, left.shape[0])
    below = dot32(right[...], upper, ((1,), (1,)))
    out_ref[:old, :old] = inverse_ref[...]
    out_ref[:old, old:] = jnp.zeros((old, left.shape[0]), jnp.float32)
    out_ref[old:, :old] = -dot32(below, inverse_ref[...], ((1,), (0,)))
    out_ref[old:, old:] = right[...]


def last_factor(inverse, gram_columns):
    total, new = gram_columns.shape
    return pl.pallas_call(
        last_factor_kernel,
        out_shape=jax.ShapeDtypeStruct((total, total), jnp.float32),
        scratch_shapes=[pltpu.VMEM((new, new), jnp.float32)] * 2,
        cost_estimate=pl.CostEstimate(flops=2 * total**3, bytes_accessed=1 << 26, transcendentals=0),
    )(inverse, gram_columns)


def body(iterate_t, vectors, old_factor_t):
    flat_iterate = iterate_t.reshape(-1, iterate_t.shape[-1])
    rows, groups = lax.axis_size("row"), lax.axis_size("col")
    column = lax.axis_index("col")
    share = vectors.shape[0]
    scale_gram = 1.0 / (rows * groups * share)

    def apply_iterate(vector, wire, filler, value):
        gathered = gather_rows(vector)
        beside = []

        def block_of(target):
            part = lax.dynamic_slice_in_dim(flat_iterate, target * share, share, 1)
            term = lax.dot_general(
                part, gathered, (((0,), (0,)), ((), ())), preferred_element_type=jnp.float32
            )
            if target is not column:
                return lax.optimization_barrier(term)
            term, late = lax.optimization_barrier((term, value))
            beside.append(filler(late))
            return term

        total = scatter_cols(block_of, column, wire)
        return lax.optimization_barrier((total, beside[0]))

    old_gathered = lax.all_gather(old_factor_t, "col", axis=0, tiled=True)
    old_full = old_gathered.astype(jnp.float32)
    old_here = lax.dynamic_slice_in_dim(old_gathered, column * share, share, 1).astype(jnp.float32)

    def old_products(old):
        return scale_gram * lax.dot_general(
            old, old, (((1,), (1,)), ((), ())), preferred_element_type=jnp.float32
        )

    first_full, old_local = apply_iterate(vectors, jnp.float32, old_products, old_gathered)
    old_old = lax.psum(old_local, "row")
    second, started = apply_iterate(first_full.astype(jnp.bfloat16), jnp.bfloat16, begin_factor, old_old)
    third, old_inverse = apply_iterate(
        second.astype(jnp.bfloat16), jnp.bfloat16, lambda pair: end_factor(*pair), started
    )
    panel = 1.5 * first_full - 0.5 * third

    old_panel = jnp.dot(old_here, panel, precision=HIGH)
    panel_panel = lax.dot_general(panel, panel, (((0,), (0,)), ((), ())), precision=HIGH)
    gram_columns = sum_all(jnp.concatenate([old_panel, panel_panel], 0) * scale_gram)
    panel_gathered = lax.all_gather(panel, "col", axis=0, tiled=True)
    inverse = last_factor(old_inverse, gram_columns)
    basis_share = inverse.shape[0] // groups
    inverse_rows = lax.dynamic_slice_in_dim(inverse, column * basis_share, basis_share, 0)
    old_count = old_gathered.shape[0]
    basis = jnp.dot(inverse_rows[:, :old_count], old_full, precision=HIGH)
    basis = basis + lax.dot_general(
        inverse_rows[:, old_count:], panel_gathered, (((1,), (1,)), ((), ())), precision=HIGH
    )
    return (panel, basis)


def solution(mesh):
    return jax.shard_map(
        body,
        mesh=mesh,
        in_specs=(P(None, "col", None, "row"), P(("row", "col"), None), P("col", "row")),
        out_specs=(P(("row", "col"), None), P("col", "row")),
        check_vma=False,
    )
```

```python
import jax
import jax.numpy as jnp
from jax import lax
from jax.experimental import pallas as pl
from jax.experimental.pallas import tpu as pltpu
from jax.sharding import PartitionSpec as P


HIGHEST = lax.Precision.HIGHEST
HIGH = lax.Precision.HIGH
TILE = 8
LANES = 128


def swap(value, axis, bit):
    size = lax.axis_size(axis)
    return lax.ppermute(value, axis, [(i, i ^ bit) for i in range(size)])


def bits_of(size, first=1):
    bits, bit = [], first
    while bit < size:
        bits.append(bit)
        bit *= 2
    return bits


def has_bit(axis, bit):
    return (lax.axis_index(axis) // bit) % 2


def join(own, other, axis, bit, dim):
    low = jnp.concatenate([own, other], dim)
    high = jnp.concatenate([other, own], dim)
    return jnp.where(has_bit(axis, bit) == 0, low, high)


def gather_rows(value, filler, late):
    size = lax.axis_size("row")
    chip_bits = bits_of(size, 2)
    half = value.shape[0] // 2
    turn = len(chip_bits) // 2
    lead = (1,) * len(chip_bits)
    parts = [value[i * half : (i + 1) * half].reshape(lead + (half, value.shape[1])) for i in range(2)]
    orders = [chip_bits, chip_bits[turn:] + chip_bits[:turn]]
    done = late
    for step in range(len(chip_bits)):
        if step == 1 and filler:
            parts, late = lax.optimization_barrier((parts, late))
            done = filler(late)
        for which in range(2):
            bit = orders[which][step]
            dim = len(chip_bits) - 1 - chip_bits.index(bit)
            parts[which] = join(parts[which], swap(parts[which], "row", bit), "row", bit, dim)
    if filler:
        parts, done = lax.optimization_barrier((parts, done))
    own = jnp.concatenate([part.reshape(size // 2, 1, 1, half, value.shape[1]) for part in parts], 2)
    return join(own, swap(own, "row", 1), "row", 1, 1).reshape(-1, value.shape[1]), done


def gather_cols(value):
    size = lax.axis_size("col")
    here = lax.axis_index("col")
    up, down = [value], [value]
    for step in range(1, size):
        up.append(lax.ppermute(up[-1], "col", [(i, i + 1) for i in range(step - 1, size - 1)]))
        down.append(lax.ppermute(down[-1], "col", [(i, i - 1) for i in range(1, size - step + 1)]))
    rows = value.shape[0]
    result = jnp.zeros((size * rows,) + value.shape[1:], value.dtype)
    for step in range(size):
        block = jnp.where(here >= step, up[step], down[size - step]) if step else value
        result = lax.dynamic_update_slice_in_dim(result, block, (here - step) % size * rows, 0)
    return result


def scatter_cols(block_of, here, wire):
    size = lax.axis_size("col")
    sums = {}

    def take(mask):
        if mask not in sums:
            sums[mask] = block_of(here ^ mask if mask else here)
        return sums[mask]

    bits = bits_of(size)
    for bit in bits:
        masks = [m for m in range(size) if m % bit == 0 and m & bit]
        for mask in sorted(masks, reverse=True):
            sent = take(mask).astype(wire)
            arrived = swap(sent, "col", bit)
            kept = take(mask ^ bit)
            sums[mask ^ bit] = kept + arrived.astype(jnp.float32)
    return take(0)


def keep_half(value, axis, bit):
    half = value.shape[0] // 2
    mine = has_bit(axis, bit)
    keep = lax.dynamic_slice_in_dim(value, mine * half, half, 0)
    send = lax.dynamic_slice_in_dim(value, (1 - mine) * half, half, 0)
    return keep + swap(send, axis, bit)


def sum_over(value, filler, late):
    size = lax.axis_size("row")
    chip_bits = bits_of(size, 2)
    turn = len(chip_bits) // 2
    mine = keep_half(value, "row", 1)
    half = mine.shape[0] // 2
    orders = [chip_bits, chip_bits[turn:] + chip_bits[:turn]]
    parts = [mine[:half], mine[half:]]
    for step in range(len(chip_bits)):
        parts = [keep_half(part, "row", order[step]) for part, order in zip(parts, orders)]
    if filler:
        both, late = lax.optimization_barrier((jnp.concatenate(parts, 0), late))
        late = filler(late)
        for bit in bits_of(lax.axis_size("col")):
            both = both + swap(both, "col", bit)
        parts = [both[: both.shape[0] // 2], both[both.shape[0] // 2 :]]
    for step in reversed(range(len(chip_bits))):
        parts = [
            join(part, swap(part, "row", order[step]), "row", order[step], 0)
            for part, order in zip(parts, orders)
        ]
    mine = jnp.concatenate(parts, 0)
    total = join(mine, swap(mine, "row", 1), "row", 1, 0)
    return (total, late) if filler else total


def eliminate(block):
    groups = LANES // TILE
    wide = (LANES, LANES)
    diagonal = lax.broadcasted_iota(jnp.int32, wide, 0) == lax.broadcasted_iota(jnp.int32, wide, 1)
    only = jnp.where(diagonal, block, 0.0)
    scale_row = 1.0 / jnp.sqrt(jnp.sum(only, axis=0, keepdims=True))
    scale_column = 1.0 / jnp.sqrt(jnp.sum(only, axis=1, keepdims=True))
    block = block * scale_row * scale_column
    start = jnp.where(diagonal, jnp.broadcast_to(scale_row, wide), 0.0)
    left = [block[g * TILE : (g + 1) * TILE] for g in range(groups)]
    right = [start[g * TILE : (g + 1) * TILE] for g in range(groups)]
    full = (TILE, LANES)
    sub = lax.broadcasted_iota(jnp.int32, full, 0)
    done = []
    for top in range(groups):
        rows = jnp.zeros(full, jnp.float32)
        for s in range(0, TILE, 2):
            j = top * TILE + s
            zero = jnp.broadcast_to(left[top][:, j : j + 1], full)
            one = jnp.broadcast_to(left[top][:, j + 1 : j + 2], full)
            p00 = jnp.broadcast_to(zero[s : s + 1], full)
            p10 = jnp.broadcast_to(zero[s + 1 : s + 2], full)
            p11 = jnp.broadcast_to(one[s + 1 : s + 2], full)
            det = p00 * p11 - p10 * p10
            inverse = 1.0 / det
            m00, m10, m11 = p11 * inverse, p10 * inverse, p00 * inverse
            l0 = jnp.broadcast_to(left[top][s : s + 1], full)
            l1 = jnp.broadcast_to(left[top][s + 1 : s + 2], full)
            r0 = jnp.broadcast_to(right[top][s : s + 1], full)
            r1 = jnp.broadcast_to(right[top][s + 1 : s + 2], full)
            lu0, lu1 = m00 * l0 - m10 * l1, m11 * l1 - m10 * l0
            ru0, ru1 = m00 * r0 - m10 * r1, m11 * r1 - m10 * r0
            for g in range(top, groups):
                if g == top:
                    c0 = jnp.where(sub > s + 1, zero, 0.0)
                    c1 = jnp.where(sub > s + 1, one, 0.0)
                else:
                    c0 = jnp.broadcast_to(left[g][:, j : j + 1], full)
                    c1 = jnp.broadcast_to(left[g][:, j + 1 : j + 2], full)
                left[g] = left[g] - (c0 * lu0 + c1 * lu1)
                right[g] = right[g] - (c0 * ru0 + c1 * ru1)
            rows = jnp.where(sub == s, r0 / jnp.sqrt(p00), rows)
            rows = jnp.where(sub == s + 1, (p00 * r1 - p10 * r0) / jnp.sqrt(p00 * det), rows)
        done.append(rows)
    return jnp.concatenate(done, 0)


def dot32(a, b, dims):
    return lax.dot_general(a, b, (dims, ((), ())), precision=HIGHEST, preferred_element_type=jnp.float32)


def invert_factor(left, right, first, last):
    size = left.shape[0]
    for start in range(first, last, LANES):
        stop = start + LANES
        diagonal = eliminate(left[start:stop, start:stop])
        right_rows = dot32(diagonal, right[start:stop, :stop], ((1,), (0,)))
        right[start:stop, :stop] = right_rows
        if stop < size:
            left_rows = dot32(diagonal, left[start:stop, stop:], ((1,), (0,)))
            left[stop:, stop:] = left[stop:, stop:] - dot32(left_rows, left_rows, ((0,), (0,)))
            right[stop:, :stop] = right[stop:, :stop] - dot32(left_rows, right_rows, ((0,), (0,)))


def identity_into(ref):
    shape = ref.shape
    ref[...] = jnp.where(
        lax.broadcasted_iota(jnp.int32, shape, 0) == lax.broadcasted_iota(jnp.int32, shape, 1), 1.0, 0.0
    )


def factor_step(state, first, last):
    if not isinstance(state, (tuple, list)):
        state = (state,)
    size = state[0].shape[0]

    def kernel(*refs):
        left, right = refs[-2:]
        left[...] = refs[0][...]
        if first == 0:
            identity_into(right)
        else:
            right[...] = refs[1][...]
        invert_factor(left, right, first, last)

    return pl.pallas_call(
        kernel,
        out_shape=[jax.ShapeDtypeStruct((size, size), jnp.float32)] * 2,
        cost_estimate=pl.CostEstimate(flops=size**3, bytes_accessed=1 << 25, transcendentals=0),
    )(*state)


def last_factor_kernel(inverse_ref, gram_ref, out_ref, left, right):
    old = inverse_ref.shape[0]
    upper = dot32(inverse_ref[...], gram_ref[:old], ((1,), (0,)))
    left[...] = gram_ref[old:] - dot32(upper, upper, ((0,), (0,)))
    identity_into(right)
    invert_factor(left, right, 0, left.shape[0])
    below = dot32(right[...], upper, ((1,), (1,)))
    out_ref[:old, :old] = inverse_ref[...]
    out_ref[:old, old:] = jnp.zeros((old, left.shape[0]), jnp.float32)
    out_ref[old:, :old] = -dot32(below, inverse_ref[...], ((1,), (0,)))
    out_ref[old:, old:] = right[...]


def last_factor(inverse, gram_columns):
    total, new = gram_columns.shape
    return pl.pallas_call(
        last_factor_kernel,
        out_shape=jax.ShapeDtypeStruct((total, total), jnp.float32),
        scratch_shapes=[pltpu.VMEM((new, new), jnp.float32)] * 2,
        cost_estimate=pl.CostEstimate(flops=2 * total**3, bytes_accessed=1 << 26, transcendentals=0),
    )(inverse, gram_columns)


def body(iterate_t, vectors, old_factor_t):
    flat_iterate = iterate_t.reshape(-1, iterate_t.shape[-1])
    rows, groups = lax.axis_size("row"), lax.axis_size("col")
    column = lax.axis_index("col")
    share = vectors.shape[0]
    scale_gram = 1.0 / (rows * groups * share)

    def apply_iterate(vector, wire, early, late, value):
        gathered, value = gather_rows(vector, early, value)
        beside = [value]

        def block_of(target):
            part = lax.dynamic_slice_in_dim(flat_iterate, target * share, share, 1)
            term = lax.dot_general(
                part, gathered, (((0,), (0,)), ((), ())), preferred_element_type=jnp.float32
            )
            if target is not column or not late:
                return lax.optimization_barrier(term)
            term, ready = lax.optimization_barrier((term, value))
            beside[0] = late(ready)
            return term

        total = scatter_cols(block_of, column, wire)
        if late:
            return lax.optimization_barrier((total, beside[0]))
        return total, value

    old_gathered = gather_cols(old_factor_t)
    old_count = old_gathered.shape[0]
    old_full = old_gathered.astype(jnp.float32)
    old_here = lax.dynamic_slice_in_dim(old_gathered, column * share, share, 1).astype(jnp.float32)
    old_local = scale_gram * lax.dot_general(
        old_gathered, old_gathered, (((1,), (1,)), ((), ())), preferred_element_type=jnp.float32
    )
    steps = [
        (lambda state, first=first: factor_step(state, first, first + old_count // 4))
        for first in range(0, old_count, old_count // 4)
    ]

    first_full, state = apply_iterate(vectors, jnp.float32, None, None, old_local)
    state = sum_over(state, None, None)
    second, state = apply_iterate(first_full.astype(jnp.bfloat16), jnp.bfloat16, None, steps[0], state)
    third, state = apply_iterate(second.astype(jnp.bfloat16), jnp.bfloat16, steps[1], steps[2], state)
    panel = 1.5 * first_full - 0.5 * third

    old_panel = jnp.dot(old_here, panel, precision=HIGH)
    panel_panel = lax.dot_general(panel, panel, (((0,), (0,)), ((), ())), precision=HIGH)
    gram_columns, state = sum_over(jnp.concatenate([old_panel, panel_panel], 0) * scale_gram, steps[3], state)
    panel_gathered = gather_cols(panel)
    inverse = last_factor(state[1], gram_columns)
    basis_share = inverse.shape[0] // groups
    inverse_rows = lax.dynamic_slice_in_dim(inverse, column * basis_share, basis_share, 0)
    basis = jnp.dot(inverse_rows[:, :old_count], old_full, precision=HIGH)
    basis = basis + lax.dot_general(
        inverse_rows[:, old_count:], panel_gathered, (((1,), (1,)), ((), ())), precision=HIGH
    )
    return (panel, basis)


def solution(mesh):
    return jax.shard_map(
        body,
        mesh=mesh,
        in_specs=(P(None, "col", None, "row"), P(("row", "col"), None), P("col", "row")),
        out_specs=(P(("row", "col"), None), P("col", "row")),
        check_vma=False,
    )
```

```python
import jax
import jax.numpy as jnp
from jax import lax
from jax.experimental import pallas as pl
from jax.experimental.pallas import tpu as pltpu
from jax.sharding import PartitionSpec as P


HIGHEST = lax.Precision.HIGHEST
HIGH = lax.Precision.HIGH
TILE = 8
LANES = 128
SCALES = 16


def swap(value, axis, bit):
    size = lax.axis_size(axis)
    return lax.ppermute(value, axis, [(i, i ^ bit) for i in range(size)])


def bits_of(size, first=1):
    bits, bit = [], first
    while bit < size:
        bits.append(bit)
        bit *= 2
    return bits


def has_bit(axis, bit):
    return (lax.axis_index(axis) // bit) % 2


def join(own, other, axis, bit, dim):
    low = jnp.concatenate([own, other], dim)
    high = jnp.concatenate([other, own], dim)
    return jnp.where(has_bit(axis, bit) == 0, low, high)


def gather_rows(value, filler, late):
    size = lax.axis_size("row")
    chip_bits = bits_of(size, 2)
    half = value.shape[0] // 2
    turn = len(chip_bits) // 2
    lead = (1,) * len(chip_bits)
    parts = [value[i * half : (i + 1) * half].reshape(lead + (half, value.shape[1])) for i in range(2)]
    orders = [chip_bits, chip_bits[turn:] + chip_bits[:turn]]
    done = late
    for step in range(len(chip_bits)):
        if step == 1 and filler:
            parts, late = lax.optimization_barrier((parts, late))
            done = filler(late)
        for which in range(2):
            bit = orders[which][step]
            dim = len(chip_bits) - 1 - chip_bits.index(bit)
            parts[which] = join(parts[which], swap(parts[which], "row", bit), "row", bit, dim)
    if filler:
        parts, done = lax.optimization_barrier((parts, done))
    own = jnp.concatenate([part.reshape(size // 2, 1, 1, half, value.shape[1]) for part in parts], 2)
    return join(own, swap(own, "row", 1), "row", 1, 1).reshape(-1, value.shape[1]), done


def pack(value):
    top = jnp.max(jnp.abs(value), axis=0, keepdims=True)
    exponent = jnp.ceil(jnp.log2(jnp.maximum(top, 1e-30)))
    scaled = (value * jnp.exp2(14.0 - exponent)).astype(jnp.float16)
    scales = jnp.broadcast_to(exponent.astype(jnp.float16), (SCALES, value.shape[1]))
    return jnp.concatenate([scaled, scales], 0)


def unpack(packed):
    size = packed.shape[-2] - SCALES
    exponent = packed[..., size : size + 1, :].astype(jnp.float32)
    return packed[..., :size, :].astype(jnp.float32) * jnp.exp2(exponent - 14.0)


def gather_cols(value):
    stacked = value[None]
    for bit in bits_of(lax.axis_size("col")):
        other = swap(stacked, "col", bit)
        stacked = join(stacked, other, "col", bit, 0)
    return stacked


def scatter_cols(block_of, here, wide):
    size = lax.axis_size("col")
    sums = {}

    def take(mask):
        if mask not in sums:
            sums[mask] = block_of(here ^ mask if mask else here)
        return sums[mask]

    bits = bits_of(size)
    for bit in bits:
        masks = [m for m in range(size) if m % bit == 0 and m & bit]
        for mask in sorted(masks, reverse=True):
            sent = pack(take(mask)) if wide else take(mask).astype(jnp.bfloat16)
            arrived = swap(sent, "col", bit)
            kept = take(mask ^ bit)
            sums[mask ^ bit] = kept + (unpack(arrived) if wide else arrived.astype(jnp.float32))
    return take(0)


def keep_half(value, axis, bit):
    half = value.shape[0] // 2
    mine = has_bit(axis, bit)
    keep = lax.dynamic_slice_in_dim(value, mine * half, half, 0)
    send = lax.dynamic_slice_in_dim(value, (1 - mine) * half, half, 0)
    return keep + swap(send, axis, bit)


def sum_over(value, filler, late):
    size = lax.axis_size("row")
    chip_bits = bits_of(size, 2)
    turn = len(chip_bits) // 2
    mine = keep_half(value, "row", 1)
    half = mine.shape[0] // 2
    orders = [chip_bits, chip_bits[turn:] + chip_bits[:turn]]
    parts = [mine[:half], mine[half:]]
    for step in range(len(chip_bits)):
        parts = [keep_half(part, "row", order[step]) for part, order in zip(parts, orders)]
    if filler:
        both = jnp.concatenate(parts, 0)
        both, late = lax.optimization_barrier((both, late))
        late = filler(late)
        for bit in bits_of(lax.axis_size("col")):
            other = swap(both, "col", bit)
            both = both + other
        parts = [both[: both.shape[0] // 2], both[both.shape[0] // 2 :]]
    for step in reversed(range(len(chip_bits))):
        parts = [
            join(part, swap(part, "row", order[step]), "row", order[step], 0)
            for part, order in zip(parts, orders)
        ]
    mine = jnp.concatenate(parts, 0)
    total = join(mine, swap(mine, "row", 1), "row", 1, 0)
    return (total, late) if filler else total


def eliminate(block):
    groups = LANES // TILE
    wide = (LANES, LANES)
    diagonal = lax.broadcasted_iota(jnp.int32, wide, 0) == lax.broadcasted_iota(jnp.int32, wide, 1)
    only = jnp.where(diagonal, block, 0.0)
    scale_row = 1.0 / jnp.sqrt(jnp.sum(only, axis=0, keepdims=True))
    scale_column = 1.0 / jnp.sqrt(jnp.sum(only, axis=1, keepdims=True))
    block = block * scale_row * scale_column
    start = jnp.where(diagonal, jnp.broadcast_to(scale_row, wide), 0.0)
    left = [block[g * TILE : (g + 1) * TILE] for g in range(groups)]
    right = [start[g * TILE : (g + 1) * TILE] for g in range(groups)]
    full = (TILE, LANES)
    sub = lax.broadcasted_iota(jnp.int32, full, 0)
    done = []
    for top in range(groups):
        rows = jnp.zeros(full, jnp.float32)
        for s in range(0, TILE, 2):
            j = top * TILE + s
            zero = jnp.broadcast_to(left[top][:, j : j + 1], full)
            one = jnp.broadcast_to(left[top][:, j + 1 : j + 2], full)
            p00 = jnp.broadcast_to(zero[s : s + 1], full)
            p10 = jnp.broadcast_to(zero[s + 1 : s + 2], full)
            p11 = jnp.broadcast_to(one[s + 1 : s + 2], full)
            det = p00 * p11 - p10 * p10
            inverse = 1.0 / det
            m00, m10, m11 = p11 * inverse, p10 * inverse, p00 * inverse
            l0 = jnp.broadcast_to(left[top][s : s + 1], full)
            l1 = jnp.broadcast_to(left[top][s + 1 : s + 2], full)
            r0 = jnp.broadcast_to(right[top][s : s + 1], full)
            r1 = jnp.broadcast_to(right[top][s + 1 : s + 2], full)
            lu0, lu1 = m00 * l0 - m10 * l1, m11 * l1 - m10 * l0
            ru0, ru1 = m00 * r0 - m10 * r1, m11 * r1 - m10 * r0
            for g in range(top, groups):
                if g == top:
                    c0 = jnp.where(sub > s + 1, zero, 0.0)
                    c1 = jnp.where(sub > s + 1, one, 0.0)
                else:
                    c0 = jnp.broadcast_to(left[g][:, j : j + 1], full)
                    c1 = jnp.broadcast_to(left[g][:, j + 1 : j + 2], full)
                left[g] = left[g] - (c0 * lu0 + c1 * lu1)
                right[g] = right[g] - (c0 * ru0 + c1 * ru1)
            rows = jnp.where(sub == s, r0 / jnp.sqrt(p00), rows)
            rows = jnp.where(sub == s + 1, (p00 * r1 - p10 * r0) / jnp.sqrt(p00 * det), rows)
        done.append(rows)
    return jnp.concatenate(done, 0)


def dot32(a, b, dims):
    return lax.dot_general(a, b, (dims, ((), ())), precision=HIGHEST, preferred_element_type=jnp.float32)


def invert_factor(left, right, first, last):
    size = left.shape[0]
    for start in range(first, last, LANES):
        stop = start + LANES
        diagonal = eliminate(left[start:stop, start:stop])
        right_rows = dot32(diagonal, right[start:stop, :stop], ((1,), (0,)))
        right[start:stop, :stop] = right_rows
        if stop < size:
            left_rows = dot32(diagonal, left[start:stop, stop:], ((1,), (0,)))
            left[stop:, stop:] = left[stop:, stop:] - dot32(left_rows, left_rows, ((0,), (0,)))
            right[stop:, :stop] = right[stop:, :stop] - dot32(left_rows, right_rows, ((0,), (0,)))


def identity_into(ref):
    shape = ref.shape
    ref[...] = jnp.where(
        lax.broadcasted_iota(jnp.int32, shape, 0) == lax.broadcasted_iota(jnp.int32, shape, 1), 1.0, 0.0
    )


def factor_step(state, first, last):
    if not isinstance(state, (tuple, list)):
        state = (state,)
    size = state[0].shape[0]

    def kernel(*refs):
        left, right = refs[-2:]
        left[...] = refs[0][...]
        if first == 0:
            identity_into(right)
        else:
            right[...] = refs[1][...]
        invert_factor(left, right, first, last)

    return pl.pallas_call(
        kernel,
        out_shape=[jax.ShapeDtypeStruct((size, size), jnp.float32)] * 2,
        cost_estimate=pl.CostEstimate(flops=size**3, bytes_accessed=1 << 25, transcendentals=0),
    )(*state)


def last_factor_kernel(inverse_ref, gram_ref, out_ref, left, right):
    old = inverse_ref.shape[0]
    upper = dot32(inverse_ref[...], gram_ref[:old], ((1,), (0,)))
    left[...] = gram_ref[old:] - dot32(upper, upper, ((0,), (0,)))
    identity_into(right)
    invert_factor(left, right, 0, left.shape[0])
    below = dot32(right[...], upper, ((1,), (1,)))
    out_ref[:old, :old] = inverse_ref[...]
    out_ref[:old, old:] = jnp.zeros((old, left.shape[0]), jnp.float32)
    out_ref[old:, :old] = -dot32(below, inverse_ref[...], ((1,), (0,)))
    out_ref[old:, old:] = right[...]


def last_factor(inverse, gram_columns):
    total, new = gram_columns.shape
    return pl.pallas_call(
        last_factor_kernel,
        out_shape=jax.ShapeDtypeStruct((total, total), jnp.float32),
        scratch_shapes=[pltpu.VMEM((new, new), jnp.float32)] * 2,
        cost_estimate=pl.CostEstimate(flops=2 * total**3, bytes_accessed=1 << 26, transcendentals=0),
    )(inverse, gram_columns)


def body(iterate_t, vectors, old_factor_t):
    flat_iterate = iterate_t.reshape(-1, iterate_t.shape[-1])
    rows, groups = lax.axis_size("row"), lax.axis_size("col")
    column = lax.axis_index("col")
    share = vectors.shape[0]
    scale_gram = 1.0 / (rows * groups * share)

    def apply_iterate(vector, wide, early, late, value):
        gathered, value = gather_rows(vector, early, value)
        beside = [value]

        def block_of(target):
            part = lax.dynamic_slice_in_dim(flat_iterate, target * share, share, 1)
            term = lax.dot_general(
                part, gathered, (((0,), (0,)), ((), ())), preferred_element_type=jnp.float32
            )
            if target is not column or not late:
                return lax.optimization_barrier(term)
            term, ready = lax.optimization_barrier((term, value))
            beside[0] = late(ready)
            return term

        total = scatter_cols(block_of, column, wide)
        if late:
            return lax.optimization_barrier((total, beside[0]))
        return total, value

    old_gathered = lax.all_gather(old_factor_t, "col", axis=0, tiled=True)
    old_count = old_gathered.shape[0]
    old_full = old_gathered.astype(jnp.float32)
    old_here = lax.dynamic_slice_in_dim(old_gathered, column * share, share, 1).astype(jnp.float32)

    def old_products(old):
        return scale_gram * lax.dot_general(
            old, old, (((1,), (1,)), ((), ())), preferred_element_type=jnp.float32
        )

    steps = [
        (lambda state, first=first: factor_step(state, first, first + old_count // 4))
        for first in range(0, old_count, old_count // 4)
    ]

    first_full, state = apply_iterate(vectors, True, None, old_products, old_gathered)
    state = lax.psum(state, "row")
    second, state = apply_iterate(first_full.astype(jnp.bfloat16), False, None, steps[0], state)
    third, state = apply_iterate(second.astype(jnp.bfloat16), False, steps[1], steps[2], state)
    panel = 1.5 * first_full - 0.5 * third

    panel, packed = lax.optimization_barrier((panel, pack(panel)))
    old_panel = jnp.dot(old_here, panel, precision=HIGH)
    panel_panel = lax.dot_general(panel, panel, (((0,), (0,)), ((), ())), precision=HIGH)
    gram_columns, state = sum_over(jnp.concatenate([old_panel, panel_panel], 0) * scale_gram, steps[3], state)
    panel_gathered = unpack(gather_cols(packed)).reshape(-1, panel.shape[1])
    inverse = last_factor(state[1], gram_columns)
    basis_share = inverse.shape[0] // groups
    inverse_rows = lax.dynamic_slice_in_dim(inverse, column * basis_share, basis_share, 0)
    basis = jnp.dot(inverse_rows[:, :old_count], old_full, precision=HIGH)
    basis = basis + lax.dot_general(
        inverse_rows[:, old_count:], panel_gathered, (((1,), (1,)), ((), ())), precision=HIGH
    )
    return (panel, basis)


def solution(mesh):
    return jax.shard_map(
        body,
        mesh=mesh,
        in_specs=(P(None, "col", None, "row"), P(("row", "col"), None), P("col", "row")),
        out_specs=(P(("row", "col"), None), P("col", "row")),
        check_vma=False,
    )
```

```python
import jax
import jax.numpy as jnp
from jax import lax
from jax.experimental import pallas as pl
from jax.experimental.pallas import tpu as pltpu
from jax.sharding import PartitionSpec as P


HIGHEST = lax.Precision.HIGHEST
HIGH = lax.Precision.HIGH
TILE = 8
LANES = 128
SCALES = 16


def swap(value, axis, bit):
    size = lax.axis_size(axis)
    return lax.ppermute(value, axis, [(i, i ^ bit) for i in range(size)])


def bits_of(size, first=1):
    bits, bit = [], first
    while bit < size:
        bits.append(bit)
        bit *= 2
    return bits


def has_bit(axis, bit):
    return (lax.axis_index(axis) // bit) % 2


def join(own, other, axis, bit, dim):
    low = jnp.concatenate([own, other], dim)
    high = jnp.concatenate([other, own], dim)
    return jnp.where(has_bit(axis, bit) == 0, low, high)


def gather_rows(value, filler, late):
    size = lax.axis_size("row")
    chip_bits = bits_of(size, 2)
    half = value.shape[0] // 2
    turn = len(chip_bits) // 2
    lead = (1,) * len(chip_bits)
    parts = [value[i * half : (i + 1) * half].reshape(lead + (half, value.shape[1])) for i in range(2)]
    orders = [chip_bits, chip_bits[turn:] + chip_bits[:turn]]
    done = late
    for step in range(len(chip_bits)):
        if step == 1 and filler:
            parts, late = lax.optimization_barrier((parts, late))
            done = filler(late)
        for which in range(2):
            bit = orders[which][step]
            dim = len(chip_bits) - 1 - chip_bits.index(bit)
            parts[which] = join(parts[which], swap(parts[which], "row", bit), "row", bit, dim)
    if filler:
        parts, done = lax.optimization_barrier((parts, done))
    own = [part.reshape(size // 2, 1, 1, half, value.shape[1]) for part in parts]
    other = [swap(part, "row", 1) for part in own]
    return join(jnp.concatenate(own, 2), jnp.concatenate(other, 2), "row", 1, 1).reshape(-1, value.shape[1]), done


def pack(value):
    top = jnp.max(jnp.abs(value), axis=0, keepdims=True)
    exponent = jnp.ceil(jnp.log2(jnp.maximum(top, 1e-30)))
    scaled = (value * jnp.exp2(14.0 - exponent)).astype(jnp.float16)
    scales = jnp.broadcast_to(exponent.astype(jnp.float16), (SCALES, value.shape[1]))
    return jnp.concatenate([scaled, scales], 0)


def unpack(packed):
    size = packed.shape[-2] - SCALES
    exponent = packed[..., size : size + 1, :].astype(jnp.float32)
    return packed[..., :size, :].astype(jnp.float32) * jnp.exp2(exponent - 14.0)


def gather_cols(value):
    stacked = value[None]
    for bit in bits_of(lax.axis_size("col")):
        other = swap(stacked, "col", bit)
        stacked = join(stacked, other, "col", bit, 0)
    return stacked


def scatter_cols(block_of, here, wide):
    size = lax.axis_size("col")
    sums = {}

    def take(mask):
        if mask not in sums:
            sums[mask] = block_of(here ^ mask if mask else here)
        return sums[mask]

    bits = bits_of(size)
    for bit in bits:
        masks = [m for m in range(size) if m % bit == 0 and m & bit]
        for mask in sorted(masks, reverse=True):
            sent = pack(take(mask)) if wide else take(mask).astype(jnp.bfloat16)
            arrived = swap(sent, "col", bit)
            kept = take(mask ^ bit)
            sums[mask ^ bit] = kept + (unpack(arrived) if wide else arrived.astype(jnp.float32))
    return take(0)


def keep_half(value, axis, bit):
    half = value.shape[0] // 2
    mine = has_bit(axis, bit)
    keep = lax.dynamic_slice_in_dim(value, mine * half, half, 0)
    send = lax.dynamic_slice_in_dim(value, (1 - mine) * half, half, 0)
    return keep + swap(send, axis, bit)


def sum_over(value, filler, late):
    size = lax.axis_size("row")
    chip_bits = bits_of(size, 2)
    turn = len(chip_bits) // 2
    mine = keep_half(value, "row", 1)
    half = mine.shape[0] // 2
    orders = [chip_bits, chip_bits[turn:] + chip_bits[:turn]]
    parts = [mine[:half], mine[half:]]
    for step in range(len(chip_bits)):
        parts = [keep_half(part, "row", order[step]) for part, order in zip(parts, orders)]
    if filler:
        both = jnp.concatenate(parts, 0)
        both, late = lax.optimization_barrier((both, late))
        late = filler(late)
        for bit in bits_of(lax.axis_size("col")):
            other = swap(both, "col", bit)
            both = both + other
        parts = [both[: both.shape[0] // 2], both[both.shape[0] // 2 :]]
    for step in reversed(range(len(chip_bits))):
        parts = [
            join(part, swap(part, "row", order[step]), "row", order[step], 0)
            for part, order in zip(parts, orders)
        ]
    mine = jnp.concatenate(parts, 0)
    total = join(mine, swap(mine, "row", 1), "row", 1, 0)
    return (total, late) if filler else total


def eliminate(block):
    groups = LANES // TILE
    wide = (LANES, LANES)
    diagonal = lax.broadcasted_iota(jnp.int32, wide, 0) == lax.broadcasted_iota(jnp.int32, wide, 1)
    only = jnp.where(diagonal, block, 0.0)
    scale_row = 1.0 / jnp.sqrt(jnp.sum(only, axis=0, keepdims=True))
    scale_column = 1.0 / jnp.sqrt(jnp.sum(only, axis=1, keepdims=True))
    block = block * scale_row * scale_column
    start = jnp.where(diagonal, jnp.broadcast_to(scale_row, wide), 0.0)
    left = [block[g * TILE : (g + 1) * TILE] for g in range(groups)]
    right = [start[g * TILE : (g + 1) * TILE] for g in range(groups)]
    full = (TILE, LANES)
    sub = lax.broadcasted_iota(jnp.int32, full, 0)
    done = []
    for top in range(groups):
        rows = jnp.zeros(full, jnp.float32)
        for s in range(0, TILE, 2):
            j = top * TILE + s
            zero = jnp.broadcast_to(left[top][:, j : j + 1], full)
            one = jnp.broadcast_to(left[top][:, j + 1 : j + 2], full)
            p00 = jnp.broadcast_to(zero[s : s + 1], full)
            p10 = jnp.broadcast_to(zero[s + 1 : s + 2], full)
            p11 = jnp.broadcast_to(one[s + 1 : s + 2], full)
            det = p00 * p11 - p10 * p10
            inverse = 1.0 / det
            m00, m10, m11 = p11 * inverse, p10 * inverse, p00 * inverse
            l0 = jnp.broadcast_to(left[top][s : s + 1], full)
            l1 = jnp.broadcast_to(left[top][s + 1 : s + 2], full)
            r0 = jnp.broadcast_to(right[top][s : s + 1], full)
            r1 = jnp.broadcast_to(right[top][s + 1 : s + 2], full)
            lu0, lu1 = m00 * l0 - m10 * l1, m11 * l1 - m10 * l0
            ru0, ru1 = m00 * r0 - m10 * r1, m11 * r1 - m10 * r0
            for g in range(top, groups):
                if g == top:
                    c0 = jnp.where(sub > s + 1, zero, 0.0)
                    c1 = jnp.where(sub > s + 1, one, 0.0)
                else:
                    c0 = jnp.broadcast_to(left[g][:, j : j + 1], full)
                    c1 = jnp.broadcast_to(left[g][:, j + 1 : j + 2], full)
                left[g] = left[g] - (c0 * lu0 + c1 * lu1)
                right[g] = right[g] - (c0 * ru0 + c1 * ru1)
            rows = jnp.where(sub == s, r0 / jnp.sqrt(p00), rows)
            rows = jnp.where(sub == s + 1, (p00 * r1 - p10 * r0) / jnp.sqrt(p00 * det), rows)
        done.append(rows)
    return jnp.concatenate(done, 0)


def dot32(a, b, dims):
    return lax.dot_general(a, b, (dims, ((), ())), precision=HIGHEST, preferred_element_type=jnp.float32)


def invert_factor(left, right, first, last):
    size = left.shape[0]
    for start in range(first, last, LANES):
        stop = start + LANES
        diagonal = eliminate(left[start:stop, start:stop])
        right_rows = dot32(diagonal, right[start:stop, :stop], ((1,), (0,)))
        right[start:stop, :stop] = right_rows
        if stop < size:
            left_rows = dot32(diagonal, left[start:stop, stop:], ((1,), (0,)))
            left[stop:, stop:] = left[stop:, stop:] - dot32(left_rows, left_rows, ((0,), (0,)))
            right[stop:, :stop] = right[stop:, :stop] - dot32(left_rows, right_rows, ((0,), (0,)))


def identity_into(ref):
    shape = ref.shape
    ref[...] = jnp.where(
        lax.broadcasted_iota(jnp.int32, shape, 0) == lax.broadcasted_iota(jnp.int32, shape, 1), 1.0, 0.0
    )


def factor_step(state, first, last):
    if not isinstance(state, (tuple, list)):
        state = (state,)
    size = state[0].shape[0]

    def kernel(*refs):
        left, right = refs[-2:]
        left[...] = refs[0][...]
        if first == 0:
            identity_into(right)
        else:
            right[...] = refs[1][...]
        invert_factor(left, right, first, last)

    return pl.pallas_call(
        kernel,
        out_shape=[jax.ShapeDtypeStruct((size, size), jnp.float32)] * 2,
        cost_estimate=pl.CostEstimate(flops=size**3, bytes_accessed=1 << 25, transcendentals=0),
    )(*state)


def last_factor_kernel(inverse_ref, gram_ref, out_ref, left, right):
    old = inverse_ref.shape[0]
    upper = dot32(inverse_ref[...], gram_ref[:old], ((1,), (0,)))
    left[...] = gram_ref[old:] - dot32(upper, upper, ((0,), (0,)))
    identity_into(right)
    invert_factor(left, right, 0, left.shape[0])
    below = dot32(right[...], upper, ((1,), (1,)))
    out_ref[:old, :old] = inverse_ref[...]
    out_ref[:old, old:] = jnp.zeros((old, left.shape[0]), jnp.float32)
    out_ref[old:, :old] = -dot32(below, inverse_ref[...], ((1,), (0,)))
    out_ref[old:, old:] = right[...]


def last_factor(inverse, gram_columns):
    total, new = gram_columns.shape
    return pl.pallas_call(
        last_factor_kernel,
        out_shape=jax.ShapeDtypeStruct((total, total), jnp.float32),
        scratch_shapes=[pltpu.VMEM((new, new), jnp.float32)] * 2,
        cost_estimate=pl.CostEstimate(flops=2 * total**3, bytes_accessed=1 << 26, transcendentals=0),
    )(inverse, gram_columns)


def body(iterate_t, vectors, old_factor_t):
    flat_iterate = iterate_t.reshape(-1, iterate_t.shape[-1])
    rows, groups = lax.axis_size("row"), lax.axis_size("col")
    column = lax.axis_index("col")
    share = vectors.shape[0]
    scale_gram = 1.0 / (rows * groups * share)

    def apply_iterate(vector, wide, early, late, value):
        gathered, value = gather_rows(vector, early, value)
        beside = [value]

        def block_of(target):
            part = lax.dynamic_slice_in_dim(flat_iterate, target * share, share, 1)
            term = lax.dot_general(
                part, gathered, (((0,), (0,)), ((), ())), preferred_element_type=jnp.float32
            )
            if target is not column or not late:
                return lax.optimization_barrier(term)
            term, ready = lax.optimization_barrier((term, value))
            beside[0] = late(ready)
            return term

        total = scatter_cols(block_of, column, wide)
        if late:
            return lax.optimization_barrier((total, beside[0]))
        return total, value

    old_gathered = lax.all_gather(old_factor_t, "col", axis=0, tiled=True)
    old_count = old_gathered.shape[0]
    old_full = old_gathered.astype(jnp.float32)
    old_here = lax.dynamic_slice_in_dim(old_gathered, column * share, share, 1).astype(jnp.float32)

    def old_products(old):
        return scale_gram * lax.dot_general(
            old, old, (((1,), (1,)), ((), ())), preferred_element_type=jnp.float32
        )

    steps = [
        (lambda state, first=first: factor_step(state, first, first + old_count // 4))
        for first in range(0, old_count, old_count // 4)
    ]

    first_full, state = apply_iterate(vectors, True, None, old_products, old_gathered)
    state = lax.psum(state, "row")
    second, state = apply_iterate(first_full.astype(jnp.bfloat16), False, None, steps[0], state)
    third, state = apply_iterate(second.astype(jnp.bfloat16), False, steps[1], steps[2], state)
    panel = 1.5 * first_full - 0.5 * third

    panel, packed = lax.optimization_barrier((panel, pack(panel)))
    old_panel = jnp.dot(old_here, panel, precision=HIGH)
    panel_panel = lax.dot_general(panel, panel, (((0,), (0,)), ((), ())), precision=HIGH)
    gram_columns, state = sum_over(jnp.concatenate([old_panel, panel_panel], 0) * scale_gram, steps[3], state)
    panel_gathered = unpack(gather_cols(packed)).reshape(-1, panel.shape[1])
    inverse = last_factor(state[1], gram_columns)
    basis_share = inverse.shape[0] // groups
    inverse_rows = lax.dynamic_slice_in_dim(inverse, column * basis_share, basis_share, 0)
    basis = jnp.dot(inverse_rows[:, :old_count], old_full, precision=HIGH)
    basis = basis + lax.dot_general(
        inverse_rows[:, old_count:], panel_gathered, (((1,), (1,)), ((), ())), precision=HIGH
    )
    return (panel, basis)


def solution(mesh):
    return jax.shard_map(
        body,
        mesh=mesh,
        in_specs=(P(None, "col", None, "row"), P(("row", "col"), None), P("col", "row")),
        out_specs=(P(("row", "col"), None), P("col", "row")),
        check_vma=False,
    )
```

```python
import jax
import jax.numpy as jnp
from jax import lax
from jax.experimental import pallas as pl
from jax.experimental.pallas import tpu as pltpu
from jax.sharding import PartitionSpec as P


HIGHEST = lax.Precision.HIGHEST
HIGH = lax.Precision.HIGH
TILE = 8
LANES = 128
SCALES = 16


def swap(value, axis, bit):
    size = lax.axis_size(axis)
    return lax.ppermute(value, axis, [(i, i ^ bit) for i in range(size)])


def bits_of(size, first=1):
    bits, bit = [], first
    while bit < size:
        bits.append(bit)
        bit *= 2
    return bits


def has_bit(axis, bit):
    return (lax.axis_index(axis) // bit) % 2


def join(own, other, axis, bit, dim):
    low = jnp.concatenate([own, other], dim)
    high = jnp.concatenate([other, own], dim)
    return jnp.where(has_bit(axis, bit) == 0, low, high)


def gather_rows(value, filler, late):
    size = lax.axis_size("row")
    chip_bits = bits_of(size, 2)
    half = value.shape[0] // 2
    turn = len(chip_bits) // 2
    lead = (1,) * len(chip_bits)
    parts = [value[i * half : (i + 1) * half].reshape(lead + (half, value.shape[1])) for i in range(2)]
    orders = [chip_bits, chip_bits[turn:] + chip_bits[:turn]]
    done = late
    for step in range(len(chip_bits)):
        if step == 1 and filler:
            parts, late = lax.optimization_barrier((parts, late))
            done = filler(late)
        for which in range(2):
            bit = orders[which][step]
            dim = len(chip_bits) - 1 - chip_bits.index(bit)
            parts[which] = join(parts[which], swap(parts[which], "row", bit), "row", bit, dim)
    if filler:
        parts, done = lax.optimization_barrier((parts, done))
    own = [part.reshape(size // 2, 1, 1, half, value.shape[1]) for part in parts]
    other = [swap(part, "row", 1) for part in own]
    return join(jnp.concatenate(own, 2), jnp.concatenate(other, 2), "row", 1, 1).reshape(-1, value.shape[1]), done


def pack(value):
    top = jnp.max(jnp.abs(value), axis=0, keepdims=True)
    exponent = jnp.ceil(jnp.log2(jnp.maximum(top, 1e-30)))
    scaled = (value * jnp.exp2(14.0 - exponent)).astype(jnp.float16)
    scales = jnp.broadcast_to(exponent.astype(jnp.float16), (SCALES, value.shape[1]))
    return jnp.concatenate([scaled, scales], 0)


def unpack(packed):
    size = packed.shape[-2] - SCALES
    exponent = packed[..., size : size + 1, :].astype(jnp.float32)
    return packed[..., :size, :].astype(jnp.float32) * jnp.exp2(exponent - 14.0)


def gather_cols(value):
    stacked = value[None]
    for bit in bits_of(lax.axis_size("col")):
        other = swap(stacked, "col", bit)
        stacked = join(stacked, other, "col", bit, 0)
    return stacked


def scatter_cols(block_of, here, wide):
    size = lax.axis_size("col")
    sums = {}

    def take(mask):
        if mask not in sums:
            sums[mask] = block_of(here ^ mask if mask else here)
        return sums[mask]

    bits = bits_of(size)
    for bit in bits:
        masks = [m for m in range(size) if m % bit == 0 and m & bit]
        for mask in sorted(masks, reverse=True):
            sent = pack(take(mask)) if wide else take(mask).astype(jnp.bfloat16)
            arrived = swap(sent, "col", bit)
            kept = take(mask ^ bit)
            sums[mask ^ bit] = kept + (unpack(arrived) if wide else arrived.astype(jnp.float32))
    return take(0)


def keep_half(value, axis, bit):
    half = value.shape[0] // 2
    mine = has_bit(axis, bit)
    keep = lax.dynamic_slice_in_dim(value, mine * half, half, 0)
    send = lax.dynamic_slice_in_dim(value, (1 - mine) * half, half, 0)
    return keep + swap(send, axis, bit)


def sum_over(value, filler, late):
    size = lax.axis_size("row")
    chip_bits = bits_of(size, 2)
    turn = len(chip_bits) // 2
    mine = keep_half(value, "row", 1)
    half = mine.shape[0] // 2
    orders = [chip_bits, chip_bits[turn:] + chip_bits[:turn]]
    parts = [mine[:half], mine[half:]]
    for step in range(len(chip_bits)):
        parts = [keep_half(part, "row", order[step]) for part, order in zip(parts, orders)]
    if filler:
        both = jnp.concatenate(parts, 0)
        both, late = lax.optimization_barrier((both, late))
        late = filler(late)
        for bit in bits_of(lax.axis_size("col")):
            other = swap(both, "col", bit)
            both = both + other
        parts = [both[: both.shape[0] // 2], both[both.shape[0] // 2 :]]
    for step in reversed(range(len(chip_bits))):
        parts = [
            join(part, swap(part, "row", order[step]), "row", order[step], 0)
            for part, order in zip(parts, orders)
        ]
    mine = jnp.concatenate(parts, 0)
    total = join(mine, swap(mine, "row", 1), "row", 1, 0)
    return (total, late) if filler else total


def eliminate(block):
    groups = LANES // TILE
    wide = (LANES, LANES)
    diagonal = lax.broadcasted_iota(jnp.int32, wide, 0) == lax.broadcasted_iota(jnp.int32, wide, 1)
    only = jnp.where(diagonal, block, 0.0)
    scale_row = 1.0 / jnp.sqrt(jnp.sum(only, axis=0, keepdims=True))
    scale_column = 1.0 / jnp.sqrt(jnp.sum(only, axis=1, keepdims=True))
    block = block * scale_row * scale_column
    start = jnp.where(diagonal, jnp.broadcast_to(scale_row, wide), 0.0)
    left = [block[g * TILE : (g + 1) * TILE] for g in range(groups)]
    right = [start[g * TILE : (g + 1) * TILE] for g in range(groups)]
    full = (TILE, LANES)
    sub = lax.broadcasted_iota(jnp.int32, full, 0)
    unit = left[0] * 0.0 + 1.0
    done = []
    for top in range(groups):
        rows = jnp.zeros(full, jnp.float32)
        for s in range(0, TILE, 2):
            j = top * TILE + s
            zero = jnp.broadcast_to(left[top][:, j : j + 1], full) * unit
            one = jnp.broadcast_to(left[top][:, j + 1 : j + 2], full) * unit
            p00 = jnp.broadcast_to(zero[s : s + 1], full)
            p10 = jnp.broadcast_to(zero[s + 1 : s + 2], full)
            p11 = jnp.broadcast_to(one[s + 1 : s + 2], full)
            det = p00 * p11 - p10 * p10
            inverse = 1.0 / det
            m00, m10, m11 = p11 * inverse, p10 * inverse, p00 * inverse
            l0 = jnp.broadcast_to(left[top][s : s + 1], full)
            l1 = jnp.broadcast_to(left[top][s + 1 : s + 2], full)
            r0 = jnp.broadcast_to(right[top][s : s + 1], full)
            r1 = jnp.broadcast_to(right[top][s + 1 : s + 2], full)
            lu0, lu1 = m00 * l0 - m10 * l1, m11 * l1 - m10 * l0
            ru0, ru1 = m00 * r0 - m10 * r1, m11 * r1 - m10 * r0
            for g in range(top, groups):
                if g == top:
                    c0 = jnp.where(sub > s + 1, zero, 0.0)
                    c1 = jnp.where(sub > s + 1, one, 0.0)
                else:
                    c0 = jnp.broadcast_to(left[g][:, j : j + 1], full)
                    c1 = jnp.broadcast_to(left[g][:, j + 1 : j + 2], full)
                left[g] = left[g] - (c0 * lu0 + c1 * lu1)
                right[g] = right[g] - (c0 * ru0 + c1 * ru1)
            rows = jnp.where(sub == s, r0 / jnp.sqrt(p00), rows)
            rows = jnp.where(sub == s + 1, (p00 * r1 - p10 * r0) / jnp.sqrt(p00 * det), rows)
        done.append(rows)
    return jnp.concatenate(done, 0)


def dot32(a, b, dims):
    return lax.dot_general(a, b, (dims, ((), ())), precision=HIGHEST, preferred_element_type=jnp.float32)


def invert_factor(left, right, first, last):
    size = left.shape[0]
    for start in range(first, last, LANES):
        stop = start + LANES
        diagonal = eliminate(left[start:stop, start:stop])
        right_rows = dot32(diagonal, right[start:stop, :stop], ((1,), (0,)))
        right[start:stop, :stop] = right_rows
        if stop < size:
            left_rows = dot32(diagonal, left[start:stop, stop:], ((1,), (0,)))
            left[stop:, stop:] = left[stop:, stop:] - dot32(left_rows, left_rows, ((0,), (0,)))
            right[stop:, :stop] = right[stop:, :stop] - dot32(left_rows, right_rows, ((0,), (0,)))


def identity_into(ref):
    shape = ref.shape
    ref[...] = jnp.where(
        lax.broadcasted_iota(jnp.int32, shape, 0) == lax.broadcasted_iota(jnp.int32, shape, 1), 1.0, 0.0
    )


def factor_step(state, first, last):
    if not isinstance(state, (tuple, list)):
        state = (state,)
    size = state[0].shape[0]

    def kernel(*refs):
        left, right = refs[-2:]
        left[...] = refs[0][...]
        if first == 0:
            identity_into(right)
        else:
            right[...] = refs[1][...]
        invert_factor(left, right, first, last)

    return pl.pallas_call(
        kernel,
        out_shape=[jax.ShapeDtypeStruct((size, size), jnp.float32)] * 2,
        cost_estimate=pl.CostEstimate(flops=size**3, bytes_accessed=1 << 25, transcendentals=0),
    )(*state)


def last_factor_kernel(inverse_ref, gram_ref, out_ref, left, right):
    old = inverse_ref.shape[0]
    upper = dot32(inverse_ref[...], gram_ref[:old], ((1,), (0,)))
    left[...] = gram_ref[old:] - dot32(upper, upper, ((0,), (0,)))
    identity_into(right)
    invert_factor(left, right, 0, left.shape[0])
    below = dot32(right[...], upper, ((1,), (1,)))
    out_ref[:old, :old] = inverse_ref[...]
    out_ref[:old, old:] = jnp.zeros((old, left.shape[0]), jnp.float32)
    out_ref[old:, :old] = -dot32(below, inverse_ref[...], ((1,), (0,)))
    out_ref[old:, old:] = right[...]


def last_factor(inverse, gram_columns):
    total, new = gram_columns.shape
    return pl.pallas_call(
        last_factor_kernel,
        out_shape=jax.ShapeDtypeStruct((total, total), jnp.float32),
        scratch_shapes=[pltpu.VMEM((new, new), jnp.float32)] * 2,
        cost_estimate=pl.CostEstimate(flops=2 * total**3, bytes_accessed=1 << 26, transcendentals=0),
    )(inverse, gram_columns)


def body(iterate_t, vectors, old_factor_t):
    flat_iterate = iterate_t.reshape(-1, iterate_t.shape[-1])
    rows, groups = lax.axis_size("row"), lax.axis_size("col")
    column = lax.axis_index("col")
    share = vectors.shape[0]
    scale_gram = 1.0 / (rows * groups * share)

    def apply_iterate(vector, wide, early, late, value):
        gathered, value = gather_rows(vector, early, value)
        beside = [value]

        def block_of(target):
            part = lax.dynamic_slice_in_dim(flat_iterate, target * share, share, 1)
            term = lax.dot_general(
                part, gathered, (((0,), (0,)), ((), ())), preferred_element_type=jnp.float32
            )
            if target is not column or not late:
                return lax.optimization_barrier(term)
            term, ready = lax.optimization_barrier((term, value))
            beside[0] = late(ready)
            return term

        total = scatter_cols(block_of, column, wide)
        if late:
            return lax.optimization_barrier((total, beside[0]))
        return total, value

    old_gathered = lax.all_gather(old_factor_t, "col", axis=0, tiled=True)
    old_count = old_gathered.shape[0]
    old_full = old_gathered.astype(jnp.float32)
    old_here = lax.dynamic_slice_in_dim(old_gathered, column * share, share, 1).astype(jnp.float32)

    def old_products(old):
        return scale_gram * lax.dot_general(
            old, old, (((1,), (1,)), ((), ())), preferred_element_type=jnp.float32
        )

    steps = [
        (lambda state, first=first: factor_step(state, first, first + old_count // 4))
        for first in range(0, old_count, old_count // 4)
    ]

    first_full, state = apply_iterate(vectors, True, None, old_products, old_gathered)
    state = lax.psum(state, "row")
    second, state = apply_iterate(first_full.astype(jnp.bfloat16), False, None, steps[0], state)
    third, state = apply_iterate(second.astype(jnp.bfloat16), False, steps[1], steps[2], state)
    panel = 1.5 * first_full - 0.5 * third

    panel, packed = lax.optimization_barrier((panel, pack(panel)))
    old_panel = jnp.dot(old_here, panel, precision=HIGH)
    panel_panel = lax.dot_general(panel, panel, (((0,), (0,)), ((), ())), precision=HIGH)
    gram_columns, state = sum_over(jnp.concatenate([old_panel, panel_panel], 0) * scale_gram, steps[3], state)
    panel_gathered = unpack(gather_cols(packed)).reshape(-1, panel.shape[1])
    inverse = last_factor(state[1], gram_columns)
    basis_share = inverse.shape[0] // groups
    inverse_rows = lax.dynamic_slice_in_dim(inverse, column * basis_share, basis_share, 0)
    basis = jnp.dot(inverse_rows[:, :old_count], old_full, precision=HIGH)
    basis = basis + lax.dot_general(
        inverse_rows[:, old_count:], panel_gathered, (((1,), (1,)), ((), ())), precision=HIGH
    )
    return (panel, basis)


def solution(mesh):
    return jax.shard_map(
        body,
        mesh=mesh,
        in_specs=(P(None, "col", None, "row"), P(("row", "col"), None), P("col", "row")),
        out_specs=(P(("row", "col"), None), P("col", "row")),
        check_vma=False,
    )
```

```python
import jax
import jax.numpy as jnp
from jax import lax
from jax.experimental import pallas as pl
from jax.experimental.pallas import tpu as pltpu
from jax.sharding import PartitionSpec as P


HIGHEST = lax.Precision.HIGHEST
HIGH = lax.Precision.HIGH
TILE = 8
LANES = 128
SCALES = 16


def swap(value, axis, bit):
    size = lax.axis_size(axis)
    return lax.ppermute(value, axis, [(i, i ^ bit) for i in range(size)])


def bits_of(size, first=1):
    bits, bit = [], first
    while bit < size:
        bits.append(bit)
        bit *= 2
    return bits


def has_bit(axis, bit):
    return (lax.axis_index(axis) // bit) % 2


def join(own, other, axis, bit, dim):
    low = jnp.concatenate([own, other], dim)
    high = jnp.concatenate([other, own], dim)
    return jnp.where(has_bit(axis, bit) == 0, low, high)


def gather_rows(value, filler, late):
    size = lax.axis_size("row")
    chip_bits = bits_of(size, 2)
    half = value.shape[0] // 2
    turn = len(chip_bits) // 2
    lead = (1,) * len(chip_bits)
    parts = [value[i * half : (i + 1) * half].reshape(lead + (half, value.shape[1])) for i in range(2)]
    orders = [chip_bits, chip_bits[turn:] + chip_bits[:turn]]
    done = late
    for step in range(len(chip_bits)):
        if step == 1 and filler:
            parts, late = lax.optimization_barrier((parts, late))
            done = filler(late)
        for which in range(2):
            bit = orders[which][step]
            dim = len(chip_bits) - 1 - chip_bits.index(bit)
            parts[which] = join(parts[which], swap(parts[which], "row", bit), "row", bit, dim)
    if filler:
        parts, _ = lax.optimization_barrier((parts, done))
    own = [part.reshape(size // 2, 1, 1, half, value.shape[1]) for part in parts]
    other = [swap(part, "row", 1) for part in own]
    return join(jnp.concatenate(own, 2), jnp.concatenate(other, 2), "row", 1, 1).reshape(-1, value.shape[1]), done


def pack(value):
    top = jnp.max(jnp.abs(value), axis=0, keepdims=True)
    exponent = jnp.ceil(jnp.log2(jnp.maximum(top, 1e-30)))
    scaled = (value * jnp.exp2(14.0 - exponent)).astype(jnp.float16)
    scales = jnp.broadcast_to(exponent.astype(jnp.float16), (SCALES, value.shape[1]))
    return jnp.concatenate([scaled, scales], 0)


def unpack(packed):
    size = packed.shape[-2] - SCALES
    exponent = packed[..., size : size + 1, :].astype(jnp.float32)
    return packed[..., :size, :].astype(jnp.float32) * jnp.exp2(exponent - 14.0)


def gather_cols(value):
    stacked = value[None]
    for bit in bits_of(lax.axis_size("col")):
        other = swap(stacked, "col", bit)
        stacked = join(stacked, other, "col", bit, 0)
    return stacked


def scatter_cols(block_of, here, wide):
    size = lax.axis_size("col")
    sums = {}

    def take(mask):
        if mask not in sums:
            sums[mask] = block_of(here ^ mask if mask else here)
        return sums[mask]

    bits = bits_of(size)
    for bit in bits:
        masks = [m for m in range(size) if m % bit == 0 and m & bit]
        for mask in sorted(masks, reverse=True):
            sent = pack(take(mask)) if wide else take(mask).astype(jnp.bfloat16)
            arrived = swap(sent, "col", bit)
            kept = take(mask ^ bit)
            sums[mask ^ bit] = kept + (unpack(arrived) if wide else arrived.astype(jnp.float32))
    return take(0)


def keep_half(value, axis, bit):
    half = value.shape[0] // 2
    mine = has_bit(axis, bit)
    keep = lax.dynamic_slice_in_dim(value, mine * half, half, 0)
    send = lax.dynamic_slice_in_dim(value, (1 - mine) * half, half, 0)
    return keep + swap(send, axis, bit)


def sum_over(value, filler, late):
    size = lax.axis_size("row")
    chip_bits = bits_of(size, 2)
    turn = len(chip_bits) // 2
    mine = keep_half(value, "row", 1)
    half = mine.shape[0] // 2
    orders = [chip_bits, chip_bits[turn:] + chip_bits[:turn]]
    parts = [mine[:half], mine[half:]]
    for step in range(len(chip_bits)):
        parts = [keep_half(part, "row", order[step]) for part, order in zip(parts, orders)]
    if filler:
        both = jnp.concatenate(parts, 0)
        both, late = lax.optimization_barrier((both, late))
        late = filler(late)
        for bit in bits_of(lax.axis_size("col")):
            other = swap(both, "col", bit)
            both = both + other
        parts = [both[: both.shape[0] // 2], both[both.shape[0] // 2 :]]
    for step in reversed(range(len(chip_bits))):
        parts = [
            join(part, swap(part, "row", order[step]), "row", order[step], 0)
            for part, order in zip(parts, orders)
        ]
    mine = jnp.concatenate(parts, 0)
    total = join(mine, swap(mine, "row", 1), "row", 1, 0)
    return (total, late) if filler else total


def eliminate(block):
    groups = LANES // TILE
    wide = (LANES, LANES)
    diagonal = lax.broadcasted_iota(jnp.int32, wide, 0) == lax.broadcasted_iota(jnp.int32, wide, 1)
    only = jnp.where(diagonal, block, 0.0)
    scale_row = 1.0 / jnp.sqrt(jnp.sum(only, axis=0, keepdims=True))
    scale_column = 1.0 / jnp.sqrt(jnp.sum(only, axis=1, keepdims=True))
    block = block * scale_row * scale_column
    start = jnp.where(diagonal, jnp.broadcast_to(scale_row, wide), 0.0)
    left = [block[g * TILE : (g + 1) * TILE] for g in range(groups)]
    right = [start[g * TILE : (g + 1) * TILE] for g in range(groups)]
    full = (TILE, LANES)
    sub = lax.broadcasted_iota(jnp.int32, full, 0)
    unit = left[0] * 0.0 + 1.0
    done = []
    for top in range(groups):
        rows = jnp.zeros(full, jnp.float32)
        for s in range(0, TILE, 2):
            j = top * TILE + s
            zero = jnp.broadcast_to(left[top][:, j : j + 1], full) * unit
            one = jnp.broadcast_to(left[top][:, j + 1 : j + 2], full) * unit
            p00 = jnp.broadcast_to(zero[s : s + 1], full)
            p10 = jnp.broadcast_to(zero[s + 1 : s + 2], full)
            p11 = jnp.broadcast_to(one[s + 1 : s + 2], full)
            det = p00 * p11 - p10 * p10
            inverse = 1.0 / det
            m00, m10, m11 = p11 * inverse, p10 * inverse, p00 * inverse
            l0 = jnp.broadcast_to(left[top][s : s + 1], full)
            l1 = jnp.broadcast_to(left[top][s + 1 : s + 2], full)
            r0 = jnp.broadcast_to(right[top][s : s + 1], full)
            r1 = jnp.broadcast_to(right[top][s + 1 : s + 2], full)
            lu0, lu1 = m00 * l0 - m10 * l1, m11 * l1 - m10 * l0
            ru0, ru1 = m00 * r0 - m10 * r1, m11 * r1 - m10 * r0
            for g in range(top, groups):
                if g == top:
                    c0 = jnp.where(sub > s + 1, zero, 0.0)
                    c1 = jnp.where(sub > s + 1, one, 0.0)
                else:
                    c0 = jnp.broadcast_to(left[g][:, j : j + 1], full)
                    c1 = jnp.broadcast_to(left[g][:, j + 1 : j + 2], full)
                left[g] = left[g] - (c0 * lu0 + c1 * lu1)
                right[g] = right[g] - (c0 * ru0 + c1 * ru1)
            rows = jnp.where(sub == s, r0 / jnp.sqrt(p00), rows)
            rows = jnp.where(sub == s + 1, (p00 * r1 - p10 * r0) / jnp.sqrt(p00 * det), rows)
        done.append(rows)
    return jnp.concatenate(done, 0)


def dot32(a, b, dims):
    return lax.dot_general(a, b, (dims, ((), ())), precision=HIGHEST, preferred_element_type=jnp.float32)


def invert_factor(left, right, first, last):
    size = left.shape[0]
    for start in range(first, last, LANES):
        stop = start + LANES
        diagonal = eliminate(left[start:stop, start:stop])
        right_rows = dot32(diagonal, right[start:stop, :stop], ((1,), (0,)))
        right[start:stop, :stop] = right_rows
        if stop < size:
            left_rows = dot32(diagonal, left[start:stop, stop:], ((1,), (0,)))
            left[stop:, stop:] = left[stop:, stop:] - dot32(left_rows, left_rows, ((0,), (0,)))
            right[stop:, :stop] = right[stop:, :stop] - dot32(left_rows, right_rows, ((0,), (0,)))


def identity_into(ref):
    shape = ref.shape
    ref[...] = jnp.where(
        lax.broadcasted_iota(jnp.int32, shape, 0) == lax.broadcasted_iota(jnp.int32, shape, 1), 1.0, 0.0
    )


def factor_step(state, first, last):
    if not isinstance(state, (tuple, list)):
        state = (state,)
    size = state[0].shape[0]

    def kernel(*refs):
        left, right = refs[-2:]
        left[...] = refs[0][...]
        if first == 0:
            identity_into(right)
        else:
            right[...] = refs[1][...]
        invert_factor(left, right, first, last)

    return pl.pallas_call(
        kernel,
        out_shape=[jax.ShapeDtypeStruct((size, size), jnp.float32)] * 2,
        cost_estimate=pl.CostEstimate(flops=size**3, bytes_accessed=1 << 25, transcendentals=0),
    )(*state)


def last_factor_kernel(inverse_ref, gram_ref, out_ref, left, right):
    old = inverse_ref.shape[0]
    upper = dot32(inverse_ref[...], gram_ref[:old], ((1,), (0,)))
    left[...] = gram_ref[old:] - dot32(upper, upper, ((0,), (0,)))
    identity_into(right)
    invert_factor(left, right, 0, left.shape[0])
    below = dot32(right[...], upper, ((1,), (1,)))
    out_ref[:old, :old] = inverse_ref[...]
    out_ref[:old, old:] = jnp.zeros((old, left.shape[0]), jnp.float32)
    out_ref[old:, :old] = -dot32(below, inverse_ref[...], ((1,), (0,)))
    out_ref[old:, old:] = right[...]


def last_factor(inverse, gram_columns):
    total, new = gram_columns.shape
    return pl.pallas_call(
        last_factor_kernel,
        out_shape=jax.ShapeDtypeStruct((total, total), jnp.float32),
        scratch_shapes=[pltpu.VMEM((new, new), jnp.float32)] * 2,
        cost_estimate=pl.CostEstimate(flops=2 * total**3, bytes_accessed=1 << 26, transcendentals=0),
    )(inverse, gram_columns)


def body(iterate_t, vectors, old_factor_t):
    flat_iterate = iterate_t.reshape(-1, iterate_t.shape[-1])
    rows, groups = lax.axis_size("row"), lax.axis_size("col")
    column = lax.axis_index("col")
    share = vectors.shape[0]
    scale_gram = 1.0 / (rows * groups * share)

    def old_products(old):
        return scale_gram * lax.dot_general(
            old, old, (((1,), (1,)), ((), ())), preferred_element_type=jnp.float32
        )

    def apply_iterate(vector, wide, early, late, value):
        gathered, value = gather_rows(vector, early, value)
        if early is old_products:
            value = lax.psum(value, "row")
        beside = [value]

        def block_of(target):
            part = lax.dynamic_slice_in_dim(flat_iterate, target * share, share, 1)
            term = lax.dot_general(
                part, gathered, (((0,), (0,)), ((), ())), preferred_element_type=jnp.float32
            )
            if target is not column or not late:
                return lax.optimization_barrier(term)
            term, ready = lax.optimization_barrier((term, value))
            beside[0] = late(ready)
            return term

        total = scatter_cols(block_of, column, wide)
        if late:
            return lax.optimization_barrier((total, beside[0]))
        return total, value

    old_gathered = lax.all_gather(old_factor_t, "col", axis=0, tiled=True)
    old_count = old_gathered.shape[0]
    old_full = old_gathered.astype(jnp.float32)
    old_here = lax.dynamic_slice_in_dim(old_gathered, column * share, share, 1).astype(jnp.float32)

    steps = [
        (lambda state, first=first: factor_step(state, first, first + old_count // 4))
        for first in range(0, old_count, old_count // 4)
    ]

    first_full, state = apply_iterate(vectors, True, None, None, old_gathered)
    second, state = apply_iterate(first_full.astype(jnp.bfloat16), False, old_products, steps[0], state)
    third, state = apply_iterate(second.astype(jnp.bfloat16), False, steps[1], steps[2], state)
    panel = 1.5 * first_full - 0.5 * third

    panel, packed = lax.optimization_barrier((panel, pack(panel)))
    old_panel = jnp.dot(old_here, panel, precision=HIGH)
    panel_panel = lax.dot_general(panel, panel, (((0,), (0,)), ((), ())), precision=HIGH)
    gram_columns, state = sum_over(jnp.concatenate([old_panel, panel_panel], 0) * scale_gram, steps[3], state)
    panel_gathered = unpack(gather_cols(packed)).reshape(-1, panel.shape[1])
    inverse = last_factor(state[1], gram_columns)
    basis_share = inverse.shape[0] // groups
    inverse_rows = lax.dynamic_slice_in_dim(inverse, column * basis_share, basis_share, 0)
    basis = jnp.dot(inverse_rows[:, :old_count], old_full, precision=HIGH)
    basis = basis + lax.dot_general(
        inverse_rows[:, old_count:], panel_gathered, (((1,), (1,)), ((), ())), precision=HIGH
    )
    return (panel, basis)


def solution(mesh):
    return jax.shard_map(
        body,
        mesh=mesh,
        in_specs=(P(None, "col", None, "row"), P(("row", "col"), None), P("col", "row")),
        out_specs=(P(("row", "col"), None), P("col", "row")),
        check_vma=False,
    )
```
